128 devices in a mesh: scan: 16 (over z_lo, x, core), tgt: 8 (over y, z_hi).
Axes of the slice: x: 4, y: 4, z: 4 (z_hi: 2, z_lo: 2; z = z_hi * 2 + z_lo), core: 2. Of those that a mesh axis runs over, the one named last changes fastest.
Arguments:
- series: bfloat16 [96, 1200, 8192], P('scan', None, 'tgt'), as said below
- seed_index: int32 [512], replicated, may hold values from 0 to 8191
Outputs:
- affinity: bfloat16 [8192, 8192], P('tgt', 'scan')
The draws below stay inside these ranges and needn't reach their ends.
Inputs may be any that keep to these rules, and one draw needn't show every extreme that they name: No grayordinate's series is constant over the frames of a scan.
All inputs are finite; a program needn't handle non-finite values.
Results may differ from the reference program's by a relative error of at most 0.0034.
Values may be sent and summed in bfloat16 or wider, within the bound.
A program may use at most 128 MiB of HBM per device.

```python
import math
import jax
import jax.numpy as jnp
from jax import lax

GRAY = 8192
SEEDS = 512
FRAMES = 1200
SCANS = 96


def draw_series(key, part):
    keys = jax.random.split(key, 9)
    networks = 12
    base_id = jax.random.randint(keys[0], (GRAY,), 0, networks)
    fresh_id = jax.random.randint(keys[7], (SCANS, GRAY), 0, networks)
    keep_draw = jax.random.randint(keys[8], (SCANS, GRAY), 0, 10)
    scan_id = jnp.where(keep_draw < 3, base_id[None, :], fresh_id)
    freq = 0.05 + 0.025 * scan_id.astype(jnp.float32)
    phase_tab = jax.random.uniform(keys[1], (SCANS, networks), jnp.float32, 0.0, 2.0 * math.pi)
    amp_tab = jnp.exp(jax.random.uniform(keys[2], (SCANS, networks), jnp.float32, math.log(0.2), math.log(3.0)))
    loading = jax.random.uniform(keys[3], (GRAY,), jnp.float32, 0.3, 1.5)
    phase_g = jnp.take_along_axis(phase_tab, scan_id, axis=1)
    amp_g = jnp.take_along_axis(amp_tab, scan_id, axis=1) * loading[None, :]
    frame_pos = jnp.arange(FRAMES, dtype=jnp.float32)
    signal = amp_g[:, None, :] * jnp.sin(freq[:, None, :] * frame_pos[None, :, None] + phase_g[:, None, :])
    noise = jax.random.normal(keys[4], (SCANS, FRAMES, GRAY), jnp.float32)
    values = signal + noise
    return values.astype(jnp.bfloat16)


def place_ends(values, own_key, least, top_value):
    longest = values.shape.index(max(values.shape))
    spots = []
    for shift in (0, 1):
        where = [jax.random.randint(jax.random.fold_in(own_key, axis), (), 0, length) for axis, length in enumerate(values.shape)]
        where[longest] = (where[longest] + shift) % values.shape[longest]
        spots.append(tuple(where))
    return values.at[spots[0]].set(least).at[spots[1]].set(top_value)


def setup_inputs(seed: int = 0) -> dict:
    key_of = jax.random.split(jax.random.key(seed), 3)
    series = draw_series(jax.random.fold_in(key_of[2], 71), 0)
    seed_index = place_ends(jax.random.randint(key_of[1], (SEEDS,), 0, GRAY), jax.random.fold_in(key_of[1], 1), 0, GRAY - 1).astype(jnp.int32)
    return dict(series=series, seed_index=seed_index)


epsilon = 1e-06
clip_level = 0.95

def fisher_map(values):
    clipped = jnp.clip(values, -clip_level, clip_level)
    return 0.5 * jnp.log((1.0 + clipped) / (1.0 - clipped))

def reference(series, seed_index):

    def one_scan(running, frames_in):
        values = frames_in.astype(jnp.float32)
        center = lax.optimization_barrier(jnp.mean(values, axis=0))
        deviate = values - center
        spread = lax.optimization_barrier(jnp.mean(deviate * deviate, axis=0))
        standard = (deviate * lax.rsqrt(spread + epsilon)).astype(jnp.bfloat16)
        seed_cols = jnp.take(standard, seed_index, axis=1)
        correl = jnp.dot(seed_cols.T, standard, preferred_element_type=jnp.float32) / FRAMES
        return (running + fisher_map(correl), None)
    profile, _ = lax.scan(one_scan, jnp.zeros((SEEDS, GRAY), jnp.float32), series)
    center = lax.optimization_barrier(jnp.mean(profile, axis=0))
    deviate = profile - center
    spread = lax.optimization_barrier(jnp.mean(deviate * deviate, axis=0))
    normal_prof = (deviate * lax.rsqrt(spread + epsilon)).astype(jnp.bfloat16)
    product = jnp.dot(normal_prof.T, normal_prof, preferred_element_type=jnp.float32)
    return jnp.tanh(product / SEEDS).astype(jnp.bfloat16)
```

```python
import jax
import jax.numpy as jnp
from jax import lax
from jax.sharding import PartitionSpec as P

epsilon = 1e-06
clip_level = 0.95
capacity = 96


def fisher_sum(correl):
    clipped = jnp.clip(correl, -clip_level, clip_level)
    above = jnp.prod(1.0 + clipped, axis=0)
    below = jnp.prod(1.0 - clipped, axis=0)
    return 0.5 * jnp.log(above / below)


def normalize_columns(profile):
    center = jnp.mean(profile, axis=0)
    deviate = profile - center
    spread = jnp.mean(deviate * deviate, axis=0)
    return (deviate * lax.rsqrt(spread + epsilon)).astype(jnp.bfloat16)


def body(series, seed_index):
    frame_count = series.shape[1]
    local_width = series.shape[2]
    seed_count = seed_index.shape[0]
    tgt_size = lax.axis_size("tgt")
    scan_size = lax.axis_size("scan")
    whole_width = local_width * tgt_size
    me = lax.axis_index("tgt")
    owner = seed_index // local_width
    local_seed = seed_index - owner * local_width
    owned = owner[:, None] == jnp.arange(tgt_size)[None, :]
    before = jnp.cumsum(owned.astype(jnp.int32), axis=0)
    count = before[-1]
    rank = jnp.sum(jnp.where(owned, before, 0), axis=1) - 1

    values = series.astype(jnp.float32)
    center = jnp.mean(values, axis=1, keepdims=True)
    deviate = values - center
    spread = jnp.mean(deviate * deviate, axis=1, keepdims=True)
    standard = (deviate * lax.rsqrt(spread + epsilon)).astype(jnp.bfloat16)

    def correlate(seed_cols):
        correl = jnp.einsum(
            "sfk,sfg->skg", seed_cols, standard, preferred_element_type=jnp.float32
        )
        return fisher_sum(correl / frame_count)

    def packed():
        mine = (owner == me)[:, None] & (rank[:, None] == jnp.arange(capacity)[None, :])
        column = jnp.sum(jnp.where(mine, local_seed[:, None] + 1, 0), axis=0) - 1
        pick = (jnp.arange(local_width)[:, None] == column[None, :]).astype(jnp.bfloat16)
        picked = jnp.einsum(
            "sfg,gk->sfk", standard, pick, preferred_element_type=jnp.float32
        ).astype(jnp.bfloat16)
        seed_cols = lax.all_gather(picked, "tgt", axis=2, tiled=True)
        return jnp.take(correlate(seed_cols), owner * capacity + rank, axis=0)

    def general():
        inside = owner == me
        picked = jnp.take(standard, local_seed, axis=2)
        picked = jnp.where(inside[None, None, :], picked, jnp.zeros_like(picked))
        return correlate(lax.psum(picked, "tgt"))

    running = lax.cond(jnp.max(count) <= capacity, packed, general)
    part = lax.psum_scatter(running, "scan", scatter_dimension=1, tiled=True)
    row_prof = lax.all_gather(normalize_columns(part), "scan", axis=1, tiled=True)
    col_width = whole_width // scan_size
    spot = lax.axis_index("scan") * col_width
    start = spot % local_width
    col_prof = lax.dynamic_slice_in_dim(row_prof, start, col_width, 1)
    col_prof = jnp.where(spot // local_width == me, col_prof, jnp.zeros_like(col_prof))
    col_prof = lax.psum(col_prof, "tgt")
    product = jnp.dot(row_prof.T, col_prof, preferred_element_type=jnp.float32)
    return jnp.tanh(product / seed_count).astype(jnp.bfloat16)


def solution(mesh):
    in_specs = (P("scan", None, "tgt"), P())
    out_specs = P("tgt", "scan")
    return jax.shard_map(body, mesh=mesh, in_specs=in_specs, out_specs=out_specs, check_vma=False)
```

```python
import functools

import jax
import jax.numpy as jnp
from jax import lax
from jax.experimental import pallas as pl
from jax.experimental.pallas import tpu as pltpu
from jax.sharding import PartitionSpec as P

epsilon = 1e-06
clip_level = 0.95
capacities = (80, 96)
MESH = pl.DeviceIdType.MESH

place_table = ((0, 2, 5, 1), (3, 6, 7, 4))


def fisher_sum(correl):
    clipped = jnp.clip(correl, -clip_level, clip_level)
    above = jnp.prod(1.0 + clipped, axis=0)
    below = jnp.prod(1.0 - clipped, axis=0)
    return 0.5 * jnp.log(above / below)


def normalize_columns(profile):
    center = jnp.mean(profile, axis=0)
    deviate = profile - center
    spread = jnp.mean(deviate * deviate, axis=0)
    return (deviate * lax.rsqrt(spread + epsilon)).astype(jnp.bfloat16)


def profile_kernel(
    cap,
    series_ref,
    pick_ref,
    out_ref,
    raw,
    standard,
    near,
    far,
    above,
    below,
    load_sem,
    send_sem,
    recv_sem,
):
    scans, frames, width = standard.shape
    me = lax.axis_index("scan")
    own = lax.axis_index("tgt")
    step = 2 - 4 * lax.rem(me, 2)
    ahead = (me, lax.rem(own + 8 + step, 8))
    behind = (me, lax.rem(own + 8 - step, 8))
    across = (me, own + 1 - 2 * lax.rem(own, 2))

    def load(s):
        slot = lax.rem(s, 2)
        return pltpu.make_async_copy(series_ref.at[s], raw.at[slot], load_sem.at[slot])

    load(0).start()
    barrier = pltpu.get_barrier_semaphore()
    for peer in (ahead, behind, across):
        pl.semaphore_signal(barrier, inc=1, device_id=peer, device_id_type=MESH)
    pl.semaphore_wait(barrier, 3)

    def rows(block):
        return pl.ds(block * cap, cap)

    flows = (
        (near, 0, near, 1, ahead),
        (near, 0, near, 2, behind),
        (near, 0, near, 3, across),
        (near, 1, far, 0, across),
        (near, 1, far, 1, ahead),
        (near, 3, far, 2, behind),
        (far, 0, far, 3, ahead),
    )

    def flow(f, s):
        source, source_block, target, target_block, peer = flows[f]
        return pltpu.make_async_remote_copy(
            src_ref=source.at[s, rows(source_block)],
            dst_ref=target.at[s, rows(target_block)],
            send_sem=send_sem.at[f, s],
            recv_sem=recv_sem.at[f, s],
            device_id=peer,
            device_id_type=MESH,
        )

    piece = 80
    pieces = frames // piece

    def fold(values):
        return jnp.sum(values.reshape(piece // 8, 8, width), axis=0)

    def standardize(s):
        slot = lax.rem(s, 2)

        def read(r):
            return raw[slot, pl.ds(r * piece, piece), :].astype(jnp.float32)

        zero = jnp.zeros((8, width), jnp.float32)
        total = lax.fori_loop(0, pieces, lambda r, acc: acc + fold(read(r)), zero)
        center = jnp.sum(total, axis=0, keepdims=True) / frames

        def squares(r, acc):
            deviate = read(r) - center
            return acc + fold(deviate * deviate)

        total = lax.fori_loop(0, pieces, squares, zero)
        spread = jnp.sum(total, axis=0, keepdims=True) / frames
        scale = lax.rsqrt(spread + epsilon)

        @pl.loop(0, pieces)
        def _(r):
            standard[s, pl.ds(r * piece, piece), :] = ((read(r) - center) * scale).astype(
                jnp.bfloat16
            )

        picked = lax.dot_general(
            pick_ref[...],
            standard[s],
            (((1,), (1,)), ((), ())),
            preferred_element_type=jnp.float32,
        )
        near[s, 0:cap, :] = picked.astype(jnp.bfloat16)

    chunk = 256

    def correlate(blocks, group, s):
        @pl.loop(0, width // chunk)
        def _(c):
            columns = pl.ds(pl.multiple_of(c * chunk, chunk), chunk)
            correl = jnp.dot(
                blocks[s], standard[s, :, columns], preferred_element_type=jnp.float32
            )
            clipped = jnp.clip(correl * (1.0 / frames), -clip_level, clip_level)
            above[group, :, columns] *= 1.0 + clipped
            below[group, :, columns] *= 1.0 - clipped

    def finish(group):
        @pl.loop(0, 4 * cap // 16)
        def _(r):
            at = pl.ds(r * 16, 16)
            out_ref[pl.ds(group * 4 * cap + r * 16, 16), :] = 0.5 * jnp.log(
                above[group, at, :] / below[group, at, :]
            )

    def body(i, carry):
        @pl.when(i < scans)
        def _():
            load(i).wait()

            @pl.when(i < scans - 1)
            def _():
                load(i + 1).start()

            standardize(i)

            @pl.when(i == 0)
            def _():
                above[...] = jnp.ones_like(above)
                below[...] = jnp.ones_like(below)

        @pl.when((i >= 2) & (i < scans + 2))
        def _():
            flow(0, i - 2).wait_recv()
            flow(3, i - 2).start()
            flow(4, i - 2).start()
            flow(2, i - 2).wait_recv()
            flow(5, i - 2).start()

        @pl.when((i >= 4) & (i < scans + 4))
        def _():
            flow(3, i - 4).wait_recv()
            flow(6, i - 4).start()

        @pl.when(i < scans)
        def _():
            for f in range(3):
                flow(f, i).start()

        @pl.when((i >= 2) & (i < scans + 2))
        def _():
            flow(1, i - 2).wait_recv()
            correlate(near, 0, i - 2)

        @pl.when(i == scans + 2)
        def _():
            finish(0)

        @pl.when(i >= 6)
        def _():
            for f in (4, 5, 6):
                flow(f, i - 6).wait_recv()
            correlate(far, 1, i - 6)

        return carry

    lax.fori_loop(0, scans + 6, body, 0)
    finish(1)

    @pl.loop(0, scans)
    def _(s):
        for f in range(7):
            flow(f, s).wait_send()


def packed_profile(cap, series, pick):
    scans, frames, width = series.shape
    return pl.pallas_call(
        functools.partial(profile_kernel, cap),
        out_shape=jax.ShapeDtypeStruct((8 * cap, width), jnp.float32),
        in_specs=[
            pl.BlockSpec(memory_space=pl.ANY),
            pl.BlockSpec(memory_space=pltpu.VMEM),
        ],
        out_specs=pl.BlockSpec(memory_space=pltpu.VMEM),
        scratch_shapes=[
            pltpu.VMEM((2, frames, width), jnp.bfloat16),
            pltpu.VMEM((scans, frames, width), jnp.bfloat16),
            pltpu.VMEM((scans, 4 * cap, frames), jnp.bfloat16),
            pltpu.VMEM((scans, 4 * cap, frames), jnp.bfloat16),
            pltpu.VMEM((2, 4 * cap, width), jnp.float32),
            pltpu.VMEM((2, 4 * cap, width), jnp.float32),
            pltpu.SemaphoreType.DMA((2,)),
            pltpu.SemaphoreType.DMA((7, scans)),
            pltpu.SemaphoreType.DMA((7, scans)),
        ],
        name="profile_%d" % cap,
        compiler_params=pltpu.CompilerParams(
            collective_id=cap, has_side_effects=True, vmem_limit_bytes=60 * 2**20
        ),
    )(series, pick)


def general_profile(series, owner, local_seed, me):
    frame_count = series.shape[1]
    values = series.astype(jnp.float32)
    center = jnp.mean(values, axis=1, keepdims=True)
    deviate = values - center
    spread = jnp.mean(deviate * deviate, axis=1, keepdims=True)
    standard = (deviate * lax.rsqrt(spread + epsilon)).astype(jnp.bfloat16)
    picked = jnp.take(standard, local_seed, axis=2)
    picked = jnp.where((owner == me)[None, None, :], picked, jnp.zeros_like(picked))
    correl = jnp.einsum(
        "sfk,sfg->skg",
        lax.psum(picked, "tgt"),
        standard,
        preferred_element_type=jnp.float32,
    )
    return fisher_sum(correl / frame_count)


def body(series, seed_index):
    local_width = series.shape[2]
    seed_count = seed_index.shape[0]
    tgt_size = lax.axis_size("tgt")
    scan_size = lax.axis_size("scan")
    whole_width = local_width * tgt_size
    me = lax.axis_index("tgt")
    owner = seed_index // local_width
    local_seed = seed_index - owner * local_width
    owned = owner[:, None] == jnp.arange(tgt_size)[None, :]
    before = jnp.cumsum(owned.astype(jnp.int32), axis=0)
    most = jnp.max(before[-1])
    rank = jnp.sum(jnp.where(owned, before, 0), axis=1) - 1
    sense = 1 - 2 * (lax.axis_index("scan") % 2)
    along = (sense * (owner // 2 - me // 2)) % 4
    place = jnp.asarray(place_table)[(owner + me) % 2, along]

    def packed(cap):
        def branch():
            mine = (owner == me)[None, :] & (
                rank[None, :] == jnp.arange(cap, dtype=jnp.int32)[:, None]
            )
            column = jnp.sum(jnp.where(mine, local_seed[None, :] + 1, 0), axis=1) - 1
            pick = (column[:, None] == jnp.arange(local_width)[None, :]).astype(jnp.bfloat16)
            profile = packed_profile(cap, series, pick)
            return jnp.take(profile, place * cap + rank, axis=0)

        return branch

    branches = [packed(cap) for cap in capacities]
    branches.append(lambda: general_profile(series, owner, local_seed, me))
    choice = sum((most > cap).astype(jnp.int32) for cap in capacities)
    running = lax.switch(choice, branches)
    part = lax.psum_scatter(running, "scan", scatter_dimension=1, tiled=True)
    row_prof = lax.all_gather(normalize_columns(part), "scan", axis=1, tiled=True)
    col_width = whole_width // scan_size
    spot = lax.axis_index("scan") * col_width
    start = spot % local_width
    col_prof = lax.dynamic_slice_in_dim(row_prof, start, col_width, 1)
    col_prof = jnp.where(spot // local_width == me, col_prof, jnp.zeros_like(col_prof))
    col_prof = lax.psum(col_prof, "tgt")
    product = jnp.dot(row_prof.T, col_prof, preferred_element_type=jnp.float32)
    return jnp.tanh(product / seed_count).astype(jnp.bfloat16)


def solution(mesh):
    in_specs = (P("scan", None, "tgt"), P())
    out_specs = P("tgt", "scan")
    return jax.shard_map(body, mesh=mesh, in_specs=in_specs, out_specs=out_specs, check_vma=False)
```

```python
import functools

import jax
import jax.numpy as jnp
from jax import lax
from jax.experimental import pallas as pl
from jax.experimental.pallas import tpu as pltpu
from jax.sharding import PartitionSpec as P

epsilon = 1e-06
clip_level = 0.95
capacities = (80, 96)
MESH = pl.DeviceIdType.MESH

place_table = ((0, 2, 5, 1), (3, 6, 7, 4))


def fisher_sum(correl):
    clipped = jnp.clip(correl, -clip_level, clip_level)
    above = jnp.prod(1.0 + clipped, axis=0)
    below = jnp.prod(1.0 - clipped, axis=0)
    return 0.5 * jnp.log(above / below)


def profile_kernel(
    cap,
    series_ref,
    pick_ref,
    out_ref,
    raw,
    standard,
    near,
    far,
    above,
    below,
    load_sem,
    send_sem,
    recv_sem,
):
    scans, frames, width = standard.shape
    me = lax.axis_index("scan")
    own = lax.axis_index("tgt")
    step = 2 - 4 * lax.rem(me, 2)
    ahead = (me, lax.rem(own + 8 + step, 8))
    behind = (me, lax.rem(own + 8 - step, 8))
    across = (me, own + 1 - 2 * lax.rem(own, 2))

    def load(s):
        slot = lax.rem(s, 2)
        return pltpu.make_async_copy(series_ref.at[s], raw.at[slot], load_sem.at[slot])

    load(0).start()
    barrier = pltpu.get_barrier_semaphore()
    for peer in (ahead, behind, across):
        pl.semaphore_signal(barrier, inc=1, device_id=peer, device_id_type=MESH)
    pl.semaphore_wait(barrier, 3)

    def rows(block):
        return pl.ds(block * cap, cap)

    flows = (
        (near, 0, near, 1, ahead),
        (near, 0, near, 2, behind),
        (near, 0, near, 3, across),
        (near, 1, far, 0, across),
        (near, 1, far, 1, ahead),
        (near, 3, far, 2, behind),
        (far, 0, far, 3, ahead),
    )

    def flow(f, s):
        source, source_block, target, target_block, peer = flows[f]
        return pltpu.make_async_remote_copy(
            src_ref=source.at[s, rows(source_block)],
            dst_ref=target.at[s, rows(target_block)],
            send_sem=send_sem.at[f, s],
            recv_sem=recv_sem.at[f, s],
            device_id=peer,
            device_id_type=MESH,
        )

    piece = 80
    pieces = frames // piece

    def fold(values):
        return jnp.sum(values.reshape(piece // 8, 8, width), axis=0)

    def standardize(s):
        slot = lax.rem(s, 2)

        def read(r):
            return raw[slot, pl.ds(r * piece, piece), :].astype(jnp.float32)

        zero = jnp.zeros((8, width), jnp.float32)
        total = lax.fori_loop(0, pieces, lambda r, acc: acc + fold(read(r)), zero)
        center = jnp.sum(total, axis=0, keepdims=True) / frames

        def squares(r, acc):
            deviate = read(r) - center
            return acc + fold(deviate * deviate)

        total = lax.fori_loop(0, pieces, squares, zero)
        spread = jnp.sum(total, axis=0, keepdims=True) / frames
        scale = lax.rsqrt(spread + epsilon)

        @pl.loop(0, pieces)
        def _(r):
            standard[s, pl.ds(r * piece, piece), :] = ((read(r) - center) * scale).astype(
                jnp.bfloat16
            )

        picked = lax.dot_general(
            pick_ref[...],
            standard[s],
            (((1,), (1,)), ((), ())),
            preferred_element_type=jnp.float32,
        )
        near[s, 0:cap, :] = picked.astype(jnp.bfloat16)

    chunk = 256

    def correlate(blocks, group, s):
        @pl.loop(0, width // chunk)
        def _(c):
            columns = pl.ds(pl.multiple_of(c * chunk, chunk), chunk)
            correl = jnp.dot(
                blocks[s], standard[s, :, columns], preferred_element_type=jnp.float32
            )
            clipped = jnp.clip(correl * (1.0 / frames), -clip_level, clip_level)
            above[group, :, columns] *= 1.0 + clipped
            below[group, :, columns] *= 1.0 - clipped

    def finish(group):
        @pl.loop(0, 4 * cap // 16)
        def _(r):
            at = pl.ds(r * 16, 16)
            out_ref[pl.ds(group * 4 * cap + r * 16, 16), :] = 0.5 * jnp.log(
                above[group, at, :] / below[group, at, :]
            )

    def body(i, carry):
        @pl.when(i < scans)
        def _():
            load(i).wait()

            @pl.when(i < scans - 1)
            def _():
                load(i + 1).start()

            standardize(i)

            @pl.when(i == 0)
            def _():
                above[...] = jnp.ones_like(above)
                below[...] = jnp.ones_like(below)

        @pl.when((i >= 2) & (i < scans + 2))
        def _():
            flow(0, i - 2).wait_recv()
            flow(3, i - 2).start()
            flow(4, i - 2).start()
            flow(2, i - 2).wait_recv()
            flow(5, i - 2).start()

        @pl.when((i >= 4) & (i < scans + 4))
        def _():
            flow(3, i - 4).wait_recv()
            flow(6, i - 4).start()

        @pl.when(i < scans)
        def _():
            for f in range(3):
                flow(f, i).start()

        @pl.when((i >= 2) & (i < scans + 2))
        def _():
            flow(1, i - 2).wait_recv()
            correlate(near, 0, i - 2)

        @pl.when(i == scans + 2)
        def _():
            finish(0)

        @pl.when(i >= 6)
        def _():
            for f in (4, 5, 6):
                flow(f, i - 6).wait_recv()
            correlate(far, 1, i - 6)

        return carry

    lax.fori_loop(0, scans + 6, body, 0)
    finish(1)

    @pl.loop(0, scans)
    def _(s):
        for f in range(7):
            flow(f, s).wait_send()


def packed_profile(cap, series, pick):
    scans, frames, width = series.shape
    return pl.pallas_call(
        functools.partial(profile_kernel, cap),
        out_shape=jax.ShapeDtypeStruct((8 * cap, width), jnp.float32),
        in_specs=[
            pl.BlockSpec(memory_space=pl.ANY),
            pl.BlockSpec(memory_space=pltpu.VMEM),
        ],
        out_specs=pl.BlockSpec(memory_space=pltpu.VMEM),
        scratch_shapes=[
            pltpu.VMEM((2, frames, width), jnp.bfloat16),
            pltpu.VMEM((scans, frames, width), jnp.bfloat16),
            pltpu.VMEM((scans, 4 * cap, frames), jnp.bfloat16),
            pltpu.VMEM((scans, 4 * cap, frames), jnp.bfloat16),
            pltpu.VMEM((2, 4 * cap, width), jnp.float32),
            pltpu.VMEM((2, 4 * cap, width), jnp.float32),
            pltpu.SemaphoreType.DMA((2,)),
            pltpu.SemaphoreType.DMA((7, scans)),
            pltpu.SemaphoreType.DMA((7, scans)),
        ],
        name="profile_%d" % cap,
        compiler_params=pltpu.CompilerParams(
            collective_id=cap, has_side_effects=True, vmem_limit_bytes=60 * 2**20
        ),
    )(series, pick)


def spread_kernel(
    run,
    row_out,
    col_out,
    swap,
    half,
    from_z,
    quarter,
    from_x,
    full,
    row,
    col,
    swap_send,
    swap_recv,
    z_send,
    z_recv,
    x_send,
    x_recv,
    join_send,
    join_recv,
    piece_send,
    piece_recv,
    tree_send,
    tree_recv,
):
    seeds, width = run.shape
    count = seeds // 2
    wide = width // 2
    lane = wide // 4
    parts = 4
    me = lax.axis_index("scan")
    own = lax.axis_index("tgt")
    core = lax.rem(me, 2)
    along_x = lax.rem(me // 2, 4)
    low = me // 8

    def turn(d):
        return lax.rem(along_x + 4 + d, 4)

    def beside(d):
        return (low * 8 + turn(d) * 2 + core, own)

    partner = (me + 1 - 2 * core, own)
    above = (lax.rem(me + 8, 16), own)
    step = 2 - 4 * core
    ahead = (me, lax.rem(own + 8 + step, 8))
    behind = (me, lax.rem(own + 8 - step, 8))
    across = (me, own + 1 - 2 * lax.rem(own, 2))

    barrier = pltpu.get_barrier_semaphore()
    for peer in (partner, above, beside(1), beside(2), beside(3), ahead, behind, across):
        pl.semaphore_signal(barrier, inc=1, device_id=peer, device_id_type=MESH)
    pl.semaphore_wait(barrier, 8)

    def remote(source, target, send, recv, peer):
        return pltpu.make_async_remote_copy(
            src_ref=source,
            dst_ref=target,
            send_sem=send,
            recv_sem=recv,
            device_id=peer,
            device_id_type=MESH,
        )

    size = count // parts
    mine = pl.multiple_of(core * count, count)
    other = pl.multiple_of(count - core * count, count)

    def rows(c):
        return pl.ds(c * size, size)

    def rows_from(base, c):
        return pl.ds(pl.multiple_of(base + c * size, size), size)

    def lanes(index, length):
        return pl.ds(pl.multiple_of(index * length, length), length)

    def swap_copy(c):
        return remote(
            run.at[rows_from(other, c)], swap.at[rows(c)], swap_send.at[c], swap_recv.at[c], partner
        )

    def z_copy(c):
        return remote(
            half.at[rows(c), lanes(1 - low, wide)],
            from_z.at[rows(c)],
            z_send.at[c],
            z_recv.at[c],
            above,
        )

    def x_copy(c, d):
        return remote(
            quarter.at[rows(c), lanes(turn(d), lane)],
            from_x.at[d - 1, rows(c)],
            x_send.at[d - 1, c],
            x_recv.at[d - 1, c],
            beside(d),
        )

    def join_copy(c):
        at = rows_from(mine, c)
        return remote(full.at[at], full.at[at], join_send.at[c], join_recv.at[c], partner)

    for c in range(parts):
        swap_copy(c).start()
    for c in range(parts):
        swap_copy(c).wait_recv()
        half[rows(c), :] = run[rows_from(mine, c), :] + swap[rows(c), :]
        z_copy(c).start()
    for c in range(parts):
        z_copy(c).wait_recv()
        quarter[rows(c), :] = half[rows(c), lanes(low, wide)] + from_z[rows(c), :]
        for d in (1, 3, 2):
            x_copy(c, d).start()
    for c in range(parts):
        for d in (1, 3, 2):
            x_copy(c, d).wait_recv()
        near = quarter[rows(c), lanes(along_x, lane)] + from_x[0, rows(c), :]
        full[rows_from(mine, c), :] = near + (from_x[1, rows(c), :] + from_x[2, rows(c), :])
        join_copy(c).start()
    for c in range(parts):
        join_copy(c).wait_recv()

    profile = full[...]
    center = jnp.sum(profile, axis=0, keepdims=True) / seeds
    deviate = profile - center
    spread = jnp.sum(deviate * deviate, axis=0, keepdims=True) / seeds
    row[:, lanes(low * 4 + along_x, lane)] = (deviate * lax.rsqrt(spread + epsilon)).astype(
        jnp.bfloat16
    )

    def piece_copy(k, index, peer):
        at = row.at[pl.ds(mine, count), lanes(index, lane)]
        return remote(at, at, piece_send.at[k], piece_recv.at[k], peer)

    def here(d):
        return low * 4 + turn(-d)

    def there(d):
        return (1 - low) * 4 + turn(-d)

    def over_x(d):
        return piece_copy(d - 1, here(0), beside(d))

    def over_z(d):
        return piece_copy(3 + d, here(d), above)

    def over_core(k):
        return piece_copy(7 + k, here(k + 1) if k < 3 else there(k - 3), partner)

    for d in (1, 3, 2):
        over_x(d).start()
    over_z(0).start()
    for d in (1, 3, 2):
        over_x(d).wait_recv()
        over_z(d).start()
        over_core(d - 1).start()
    for d in (0, 1, 3, 2):
        over_z(d).wait_recv()
        over_core(3 + d).start()
    for k in (0, 2, 1, 3, 4, 6, 5):
        over_core(k).wait_recv()

    root = me // 2
    sense = 1 - 2 * core
    far_y = lax.rem(sense * (own // 2 - root // 2) + 8, 4)
    same_z = lax.rem(own + root, 2) == 0
    is_root = (far_y == 0) & same_z
    sends_on = far_y < 2
    bulk = seeds // parts

    def tree_copy(kind, c):
        at = col.at[pl.ds(c * bulk, bulk)]
        peer = (ahead, behind, across)[kind]
        return remote(at, at, tree_send.at[kind, c], tree_recv.at[c], peer)

    @pl.when(is_root)
    def _():
        col[...] = row[:, lanes(core, wide)]

    for c in range(parts):

        @pl.when(jnp.logical_not(is_root))
        def _():
            tree_copy(0, c).wait_recv()

        @pl.when(is_root)
        def _():
            tree_copy(2, c).start()

        @pl.when(sends_on)
        def _():
            tree_copy(0, c).start()

        @pl.when(far_y == 0)
        def _():
            tree_copy(1, c).start()

    row_out[...] = row[...]
    col_out[...] = col[...]

    for c in range(parts):
        swap_copy(c).wait_send()
        z_copy(c).wait_send()
        for d in (1, 2, 3):
            x_copy(c, d).wait_send()
        join_copy(c).wait_send()
    for d in (1, 2, 3):
        over_x(d).wait_send()
    for d in range(4):
        over_z(d).wait_send()
    for k in range(7):
        over_core(k).wait_send()
    for c in range(parts):

        @pl.when(is_root)
        def _():
            tree_copy(2, c).wait_send()

        @pl.when(sends_on)
        def _():
            tree_copy(0, c).wait_send()

        @pl.when(far_y == 0)
        def _():
            tree_copy(1, c).wait_send()


def spread_profiles(running, col_width):
    seeds, width = running.shape
    count, wide, lane = seeds // 2, width // 2, width // 8
    dma = pltpu.SemaphoreType.DMA
    whole = pl.BlockSpec(memory_space=pltpu.VMEM)
    return pl.pallas_call(
        spread_kernel,
        out_shape=(
            jax.ShapeDtypeStruct((seeds, width), jnp.bfloat16),
            jax.ShapeDtypeStruct((seeds, col_width), jnp.bfloat16),
        ),
        in_specs=[whole],
        out_specs=(whole, whole),
        scratch_shapes=[
            pltpu.VMEM((count, width), jnp.float32),
            pltpu.VMEM((count, width), jnp.float32),
            pltpu.VMEM((count, wide), jnp.float32),
            pltpu.VMEM((count, wide), jnp.float32),
            pltpu.VMEM((3, count, lane), jnp.float32),
            pltpu.VMEM((seeds, lane), jnp.float32),
            pltpu.VMEM((seeds, width), jnp.bfloat16),
            pltpu.VMEM((seeds, col_width), jnp.bfloat16),
            dma((4,)),
            dma((4,)),
            dma((4,)),
            dma((4,)),
            dma((3, 4)),
            dma((3, 4)),
            dma((4,)),
            dma((4,)),
            dma((14,)),
            dma((14,)),
            dma((3, 4)),
            dma((4,)),
        ],
        name="spread",
        compiler_params=pltpu.CompilerParams(collective_id=1, has_side_effects=True),
    )(running)


def general_profile(series, owner, local_seed, me):
    frame_count = series.shape[1]
    values = series.astype(jnp.float32)
    center = jnp.mean(values, axis=1, keepdims=True)
    deviate = values - center
    spread = jnp.mean(deviate * deviate, axis=1, keepdims=True)
    standard = (deviate * lax.rsqrt(spread + epsilon)).astype(jnp.bfloat16)
    picked = jnp.take(standard, local_seed, axis=2)
    picked = jnp.where((owner == me)[None, None, :], picked, jnp.zeros_like(picked))
    correl = jnp.einsum(
        "sfk,sfg->skg",
        lax.psum(picked, "tgt"),
        standard,
        preferred_element_type=jnp.float32,
    )
    return fisher_sum(correl / frame_count)


def body(series, seed_index):
    local_width = series.shape[2]
    seed_count = seed_index.shape[0]
    tgt_size = lax.axis_size("tgt")
    scan_size = lax.axis_size("scan")
    whole_width = local_width * tgt_size
    me = lax.axis_index("tgt")
    owner = seed_index // local_width
    local_seed = seed_index - owner * local_width
    owned = owner[:, None] == jnp.arange(tgt_size)[None, :]
    before = jnp.cumsum(owned.astype(jnp.int32), axis=0)
    most = jnp.max(before[-1])
    rank = jnp.sum(jnp.where(owned, before, 0), axis=1) - 1
    sense = 1 - 2 * (lax.axis_index("scan") % 2)
    along = (sense * (owner // 2 - me // 2)) % 4
    place = jnp.asarray(place_table)[(owner + me) % 2, along]

    def packed(cap):
        def branch():
            mine = (owner == me)[None, :] & (
                rank[None, :] == jnp.arange(cap, dtype=jnp.int32)[:, None]
            )
            column = jnp.sum(jnp.where(mine, local_seed[None, :] + 1, 0), axis=1) - 1
            pick = (column[:, None] == jnp.arange(local_width)[None, :]).astype(jnp.bfloat16)
            profile = packed_profile(cap, series, pick)
            return jnp.take(profile, place * cap + rank, axis=0)

        return branch

    branches = [packed(cap) for cap in capacities]
    branches.append(lambda: general_profile(series, owner, local_seed, me))
    choice = sum((most > cap).astype(jnp.int32) for cap in capacities)
    running = lax.switch(choice, branches)
    row_prof, col_prof = spread_profiles(running, whole_width // scan_size)
    product = jnp.dot(row_prof.T, col_prof, preferred_element_type=jnp.float32)
    return jnp.tanh(product / seed_count).astype(jnp.bfloat16)


def solution(mesh):
    in_specs = (P("scan", None, "tgt"), P())
    out_specs = P("tgt", "scan")
    return jax.shard_map(body, mesh=mesh, in_specs=in_specs, out_specs=out_specs, check_vma=False)
```

```python
import functools

import jax
import jax.numpy as jnp
from jax import lax
from jax.experimental import pallas as pl
from jax.experimental.pallas import tpu as pltpu
from jax.sharding import PartitionSpec as P

epsilon = 1e-06
clip_level = 0.95
capacities = (80, 96)
MESH = pl.DeviceIdType.MESH

place_table = ((0, 2, 5, 1), (3, 6, 7, 4))


def fisher_sum(correl):
    clipped = jnp.clip(correl, -clip_level, clip_level)
    above = jnp.prod(1.0 + clipped, axis=0)
    below = jnp.prod(1.0 - clipped, axis=0)
    return 0.5 * jnp.log(above / below)


def profile_kernel(
    cap,
    series_ref,
    pick_ref,
    out_ref,
    raw,
    standard,
    near,
    far,
    above,
    below,
    load_sem,
    send_sem,
    recv_sem,
):
    scans, frames, width = standard.shape
    me = lax.axis_index("scan")
    own = lax.axis_index("tgt")
    step = 2 - 4 * lax.rem(me, 2)
    ahead = (me, lax.rem(own + 8 + step, 8))
    behind = (me, lax.rem(own + 8 - step, 8))
    across = (me, own + 1 - 2 * lax.rem(own, 2))

    def load(s):
        slot = lax.rem(s, 2)
        return pltpu.make_async_copy(series_ref.at[s], raw.at[slot], load_sem.at[slot])

    load(0).start()
    barrier = pltpu.get_barrier_semaphore()
    for peer in (ahead, behind, across):
        pl.semaphore_signal(barrier, inc=1, device_id=peer, device_id_type=MESH)
    pl.semaphore_wait(barrier, 3)

    def rows(block):
        return pl.ds(block * cap, cap)

    flows = (
        (near, 0, near, 1, ahead),
        (near, 0, near, 2, behind),
        (near, 0, near, 3, across),
        (near, 1, far, 0, across),
        (near, 1, far, 1, ahead),
        (near, 3, far, 2, behind),
        (far, 0, far, 3, ahead),
    )

    def flow(f, s):
        source, source_block, target, target_block, peer = flows[f]
        return pltpu.make_async_remote_copy(
            src_ref=source.at[s, rows(source_block)],
            dst_ref=target.at[s, rows(target_block)],
            send_sem=send_sem.at[f, s],
            recv_sem=recv_sem.at[f, s],
            device_id=peer,
            device_id_type=MESH,
        )

    piece = 80
    pieces = frames // piece

    def fold(values):
        return jnp.sum(values.reshape(piece // 8, 8, width), axis=0)

    def standardize(s):
        slot = lax.rem(s, 2)

        def read(r):
            return raw[slot, pl.ds(r * piece, piece), :].astype(jnp.float32)

        zero = jnp.zeros((8, width), jnp.float32)
        total = lax.fori_loop(0, pieces, lambda r, acc: acc + fold(read(r)), zero)
        center = jnp.sum(total, axis=0, keepdims=True) / frames

        def squares(r, acc):
            deviate = read(r) - center
            return acc + fold(deviate * deviate)

        total = lax.fori_loop(0, pieces, squares, zero)
        spread = jnp.sum(total, axis=0, keepdims=True) / frames
        scale = lax.rsqrt(spread + epsilon)

        @pl.loop(0, pieces)
        def _(r):
            standard[s, pl.ds(r * piece, piece), :] = ((read(r) - center) * scale).astype(
                jnp.bfloat16
            )

        picked = lax.dot_general(
            pick_ref[...],
            standard[s],
            (((1,), (1,)), ((), ())),
            preferred_element_type=jnp.float32,
        )
        near[s, 0:cap, :] = picked.astype(jnp.bfloat16)

    chunk = 256

    def correlate(blocks, group, s):
        @pl.loop(0, width // chunk)
        def _(c):
            columns = pl.ds(pl.multiple_of(c * chunk, chunk), chunk)
            correl = jnp.dot(
                blocks[s], standard[s, :, columns], preferred_element_type=jnp.float32
            )
            clipped = jnp.clip(correl * (1.0 / frames), -clip_level, clip_level)
            above[group, :, columns] *= 1.0 + clipped
            below[group, :, columns] *= 1.0 - clipped

    def finish(group):
        @pl.loop(0, 4 * cap // 16)
        def _(r):
            at = pl.ds(r * 16, 16)
            out_ref[pl.ds(group * 4 * cap + r * 16, 16), :] = 0.5 * jnp.log(
                above[group, at, :] / below[group, at, :]
            )

    def body(i, carry):
        @pl.when(i < scans)
        def _():
            load(i).wait()

            @pl.when(i < scans - 1)
            def _():
                load(i + 1).start()

            standardize(i)

            @pl.when(i == 0)
            def _():
                above[...] = jnp.ones_like(above)
                below[...] = jnp.ones_like(below)

        @pl.when((i >= 2) & (i < scans + 2))
        def _():
            flow(0, i - 2).wait_recv()
            flow(3, i - 2).start()
            flow(4, i - 2).start()
            flow(2, i - 2).wait_recv()
            flow(5, i - 2).start()

        @pl.when((i >= 4) & (i < scans + 4))
        def _():
            flow(3, i - 4).wait_recv()
            flow(6, i - 4).start()

        @pl.when(i < scans)
        def _():
            for f in range(3):
                flow(f, i).start()

        @pl.when((i >= 2) & (i < scans + 2))
        def _():
            flow(1, i - 2).wait_recv()
            correlate(near, 0, i - 2)

        @pl.when(i == scans + 2)
        def _():
            finish(0)

        @pl.when(i >= 6)
        def _():
            for f in (4, 5, 6):
                flow(f, i - 6).wait_recv()
            correlate(far, 1, i - 6)

        return carry

    lax.fori_loop(0, scans + 6, body, 0)
    finish(1)

    @pl.loop(0, scans)
    def _(s):
        for f in range(7):
            flow(f, s).wait_send()


def packed_profile(cap, series, pick):
    scans, frames, width = series.shape
    return pl.pallas_call(
        functools.partial(profile_kernel, cap),
        out_shape=jax.ShapeDtypeStruct((8 * cap, width), jnp.float32),
        in_specs=[
            pl.BlockSpec(memory_space=pl.ANY),
            pl.BlockSpec(memory_space=pltpu.VMEM),
        ],
        out_specs=pl.BlockSpec(memory_space=pltpu.VMEM),
        scratch_shapes=[
            pltpu.VMEM((2, frames, width), jnp.bfloat16),
            pltpu.VMEM((scans, frames, width), jnp.bfloat16),
            pltpu.VMEM((scans, 4 * cap, frames), jnp.bfloat16),
            pltpu.VMEM((scans, 4 * cap, frames), jnp.bfloat16),
            pltpu.VMEM((2, 4 * cap, width), jnp.float32),
            pltpu.VMEM((2, 4 * cap, width), jnp.float32),
            pltpu.SemaphoreType.DMA((2,)),
            pltpu.SemaphoreType.DMA((7, scans)),
            pltpu.SemaphoreType.DMA((7, scans)),
        ],
        name="profile_%d" % cap,
        compiler_params=pltpu.CompilerParams(
            collective_id=cap, has_side_effects=True, vmem_limit_bytes=60 * 2**20
        ),
    )(series, pick)


def spread_kernel(
    run,
    row_out,
    col_out,
    swap,
    half,
    from_z,
    quarter,
    from_x,
    full,
    row,
    col,
    swap_send,
    swap_recv,
    z_send,
    z_recv,
    x_send,
    x_recv,
    join_send,
    join_recv,
    piece_send,
    piece_recv,
    tree_send,
    tree_recv,
):
    seeds, width = run.shape
    count = seeds // 2
    wide = width // 2
    lane = wide // 4
    parts = 4
    me = lax.axis_index("scan")
    own = lax.axis_index("tgt")
    core = lax.rem(me, 2)
    along_x = lax.rem(me // 2, 4)
    low = me // 8

    def turn(d):
        return lax.rem(along_x + 4 + d, 4)

    def beside(d):
        return (low * 8 + turn(d) * 2 + core, own)

    partner = (me + 1 - 2 * core, own)
    above = (lax.rem(me + 8, 16), own)
    step = 2 - 4 * core
    ahead = (me, lax.rem(own + 8 + step, 8))
    behind = (me, lax.rem(own + 8 - step, 8))
    across = (me, own + 1 - 2 * lax.rem(own, 2))

    barrier = pltpu.get_barrier_semaphore()
    for peer in (partner, above, beside(1), beside(2), beside(3), ahead, behind, across):
        pl.semaphore_signal(barrier, inc=1, device_id=peer, device_id_type=MESH)
    pl.semaphore_wait(barrier, 8)

    def remote(source, target, send, recv, peer):
        return pltpu.make_async_remote_copy(
            src_ref=source,
            dst_ref=target,
            send_sem=send,
            recv_sem=recv,
            device_id=peer,
            device_id_type=MESH,
        )

    size = count // parts
    mine = pl.multiple_of(core * count, count)
    other = pl.multiple_of(count - core * count, count)

    def rows(c):
        return pl.ds(c * size, size)

    def rows_from(base, c):
        return pl.ds(pl.multiple_of(base + c * size, size), size)

    def lanes(index, length):
        return pl.ds(pl.multiple_of(index * length, length), length)

    def swap_copy(c):
        return remote(
            run.at[rows_from(other, c)], swap.at[rows(c)], swap_send.at[c], swap_recv.at[c], partner
        )

    def z_copy(c):
        return remote(
            half.at[rows(c), lanes(1 - low, wide)],
            from_z.at[rows(c)],
            z_send.at[c],
            z_recv.at[c],
            above,
        )

    def x_copy(c, d):
        return remote(
            quarter.at[rows(c), lanes(turn(d), lane)],
            from_x.at[d - 1, rows(c)],
            x_send.at[d - 1, c],
            x_recv.at[d - 1, c],
            beside(d),
        )

    def join_copy(c):
        at = rows_from(mine, c)
        return remote(full.at[at], full.at[at], join_send.at[c], join_recv.at[c], partner)

    for c in range(parts):
        swap_copy(c).start()
    for c in range(parts):
        swap_copy(c).wait_recv()
        half[rows(c), :] = run[rows_from(mine, c), :] + swap[rows(c), :]
        z_copy(c).start()
    for c in range(parts):
        z_copy(c).wait_recv()
        quarter[rows(c), :] = half[rows(c), lanes(low, wide)] + from_z[rows(c), :]
        for d in (1, 3, 2):
            x_copy(c, d).start()
    for c in range(parts):
        for d in (1, 3, 2):
            x_copy(c, d).wait_recv()
        near = quarter[rows(c), lanes(along_x, lane)] + from_x[0, rows(c), :]
        full[rows_from(mine, c), :] = near + (from_x[1, rows(c), :] + from_x[2, rows(c), :])
        join_copy(c).start()
    for c in range(parts):
        join_copy(c).wait_recv()

    profile = full[...]
    center = jnp.sum(profile, axis=0, keepdims=True) / seeds
    deviate = profile - center
    spread = jnp.sum(deviate * deviate, axis=0, keepdims=True) / seeds
    row[:, lanes(low * 4 + along_x, lane)] = (deviate * lax.rsqrt(spread + epsilon)).astype(
        jnp.bfloat16
    )

    def piece_copy(k, index, peer):
        at = row.at[pl.ds(mine, count), lanes(index, lane)]
        return remote(at, at, piece_send.at[k], piece_recv.at[k], peer)

    def here(d):
        return low * 4 + turn(-d)

    def there(d):
        return (1 - low) * 4 + turn(-d)

    def over_x(d):
        return piece_copy(d - 1, here(0), beside(d))

    def over_z(d):
        return piece_copy(3 + d, here(d), above)

    def over_core(k):
        return piece_copy(7 + k, here(k + 1) if k < 3 else there(k - 3), partner)

    for d in (1, 3, 2):
        over_x(d).start()
    over_z(0).start()
    for d in (1, 3, 2):
        over_x(d).wait_recv()
        over_z(d).start()
        over_core(d - 1).start()
    for d in (0, 1, 3, 2):
        over_z(d).wait_recv()
        over_core(3 + d).start()
    for k in (0, 2, 1, 3, 4, 6, 5):
        over_core(k).wait_recv()

    root = me // 2
    sense = 1 - 2 * core
    far_y = lax.rem(sense * (own // 2 - root // 2) + 8, 4)
    same_z = lax.rem(own + root, 2) == 0
    is_root = (far_y == 0) & same_z
    sends_on = far_y < 2
    bulk = seeds // parts

    def tree_copy(kind, c):
        at = col.at[pl.ds(c * bulk, bulk)]
        peer = (ahead, behind, across)[kind]
        return remote(at, at, tree_send.at[kind, c], tree_recv.at[c], peer)

    @pl.when(is_root)
    def _():
        col[...] = row[:, lanes(core, wide)]

    for c in range(parts):

        @pl.when(jnp.logical_not(is_root))
        def _():
            tree_copy(0, c).wait_recv()

        @pl.when(is_root)
        def _():
            tree_copy(2, c).start()

        @pl.when(sends_on)
        def _():
            tree_copy(0, c).start()

        @pl.when(far_y == 0)
        def _():
            tree_copy(1, c).start()

    row_out[...] = row[...]
    col_out[...] = col[...]

    for c in range(parts):
        swap_copy(c).wait_send()
        z_copy(c).wait_send()
        for d in (1, 2, 3):
            x_copy(c, d).wait_send()
        join_copy(c).wait_send()
    for d in (1, 2, 3):
        over_x(d).wait_send()
    for d in range(4):
        over_z(d).wait_send()
    for k in range(7):
        over_core(k).wait_send()
    for c in range(parts):

        @pl.when(is_root)
        def _():
            tree_copy(2, c).wait_send()

        @pl.when(sends_on)
        def _():
            tree_copy(0, c).wait_send()

        @pl.when(far_y == 0)
        def _():
            tree_copy(1, c).wait_send()


def spread_profiles(running, col_width):
    seeds, width = running.shape
    count, wide, lane = seeds // 2, width // 2, width // 8
    dma = pltpu.SemaphoreType.DMA
    whole = pl.BlockSpec(memory_space=pltpu.VMEM)
    return pl.pallas_call(
        spread_kernel,
        out_shape=(
            jax.ShapeDtypeStruct((seeds, width), jnp.bfloat16),
            jax.ShapeDtypeStruct((seeds, col_width), jnp.bfloat16),
        ),
        in_specs=[whole],
        out_specs=(whole, whole),
        scratch_shapes=[
            pltpu.VMEM((count, width), jnp.float32),
            pltpu.VMEM((count, width), jnp.float32),
            pltpu.VMEM((count, wide), jnp.float32),
            pltpu.VMEM((count, wide), jnp.float32),
            pltpu.VMEM((3, count, lane), jnp.float32),
            pltpu.VMEM((seeds, lane), jnp.float32),
            pltpu.VMEM((seeds, width), jnp.bfloat16),
            pltpu.VMEM((seeds, col_width), jnp.bfloat16),
            dma((4,)),
            dma((4,)),
            dma((4,)),
            dma((4,)),
            dma((3, 4)),
            dma((3, 4)),
            dma((4,)),
            dma((4,)),
            dma((14,)),
            dma((14,)),
            dma((3, 4)),
            dma((4,)),
        ],
        name="spread",
        compiler_params=pltpu.CompilerParams(collective_id=1, has_side_effects=True),
    )(running)


def general_profile(series, owner, local_seed, me):
    frame_count = series.shape[1]
    values = series.astype(jnp.float32)
    center = jnp.mean(values, axis=1, keepdims=True)
    deviate = values - center
    spread = jnp.mean(deviate * deviate, axis=1, keepdims=True)
    standard = (deviate * lax.rsqrt(spread + epsilon)).astype(jnp.bfloat16)
    picked = jnp.take(standard, local_seed, axis=2)
    picked = jnp.where((owner == me)[None, None, :], picked, jnp.zeros_like(picked))
    size = lax.axis_size("tgt")
    ring = [(i, (i + 1) % size) for i in range(size)]

    def hop(_, state):
        moving, total = state
        moving = lax.ppermute(moving, "tgt", ring)
        return moving, total + moving

    gathered = lax.fori_loop(0, size - 1, hop, (picked, picked))[1]
    correl = jnp.einsum(
        "sfk,sfg->skg",
        gathered,
        standard,
        preferred_element_type=jnp.float32,
    )
    return fisher_sum(correl / frame_count)


def body(series, seed_index):
    local_width = series.shape[2]
    seed_count = seed_index.shape[0]
    tgt_size = lax.axis_size("tgt")
    scan_size = lax.axis_size("scan")
    whole_width = local_width * tgt_size
    me = lax.axis_index("tgt")
    owner = seed_index // local_width
    local_seed = seed_index - owner * local_width
    owned = owner[:, None] == jnp.arange(tgt_size)[None, :]
    before = jnp.cumsum(owned.astype(jnp.int32), axis=0)
    most = jnp.max(before[-1])
    rank = jnp.sum(jnp.where(owned, before, 0), axis=1) - 1
    sense = 1 - 2 * (lax.axis_index("scan") % 2)
    along = (sense * (owner // 2 - me // 2)) % 4
    code = (owner + me) % 2 * 4 + along
    place = sum(
        jnp.where(code == at, block, 0)
        for at, block in enumerate(place_table[0] + place_table[1])
    )

    def packed(cap):
        def branch():
            mine = (owner == me)[None, :] & (
                rank[None, :] == jnp.arange(cap, dtype=jnp.int32)[:, None]
            )
            column = jnp.sum(jnp.where(mine, local_seed[None, :] + 1, 0), axis=1) - 1
            pick = (column[:, None] == jnp.arange(local_width)[None, :]).astype(jnp.bfloat16)
            profile = packed_profile(cap, series, pick)
            return profile.at[place * cap + rank].get(mode="promise_in_bounds")

        return branch

    branches = [packed(cap) for cap in capacities]
    branches.append(lambda: general_profile(series, owner, local_seed, me))
    choice = sum((most > cap).astype(jnp.int32) for cap in capacities)
    running = lax.switch(choice, branches)
    row_prof, col_prof = spread_profiles(running, whole_width // scan_size)
    product = jnp.dot(row_prof.T, col_prof, preferred_element_type=jnp.float32)
    return jnp.tanh(product / seed_count).astype(jnp.bfloat16)


def solution(mesh):
    in_specs = (P("scan", None, "tgt"), P())
    out_specs = P("tgt", "scan")
    return jax.shard_map(body, mesh=mesh, in_specs=in_specs, out_specs=out_specs, check_vma=False)
```
